512 devices in a mesh: space: 64 (over y, z), spec: 8 (over x, core).
Axes of the slice: x: 4, y: 4, z: 16, core: 2. Of those that a mesh axis runs over, the one named last changes fastest.
Arguments:
- action: float32 [24, 36, 2048, 128], P('spec', None, 'space'), may hold values from 0.1 to 1
- courant: float32 [24], P('spec'), may hold values from 0.1 to 0.6
- bending: float32 [2048, 128], P('space'), may hold values from -0.25 to 0.25
- land_mask: int32 [2048, 128], P('space'), may hold values 0 or 1
- friction: float32 [2048, 128], P(('space', 'spec')), may hold values from 0.5 to 2
- wind_dir: float32 [2048, 128], P(('space', 'spec')), may hold values from -3.140625 to 3.140625
Outputs:
- wave_out: float32 [24, 36, 2048, 128], P('spec', None, 'space')
The draws below stay inside these ranges and needn't reach their ends.
Inputs may be any that keep to these rules, and one draw needn't show every extreme that they name: `land_mask`: 1 marks land.
All inputs are finite; a program needn't handle non-finite values. No bound on the sum of `land_mask` on one device may be relied on, other than what follows from the above.
Results may differ from the reference program's by a relative error of at most 0.00002.
Values sent between devices are 32-bit elements; how exact they have to be, the bound alone decides.
No kernel may reach another device: no remote copies, remote signals or barrier semaphores. Data moves between devices by JAX's collectives and lax.ppermute only.
A program may use at most 64 MiB of HBM per device.

```python
import math
import jax
import jax.numpy as jnp
from jax import lax

DIRS = 36
NR = 128
ITERS = 8
NF = 24
NX = 2048


def set_ends(array, stream_key, low, largest):
    spot = [jax.random.randint(jax.random.fold_in(stream_key, axis), (), 0, length) for axis, length in enumerate(array.shape)]
    main_axis = array.shape.index(max(array.shape))
    next_to = spot[:main_axis] + [(spot[main_axis] + 1) % array.shape[main_axis]] + spot[main_axis + 1:]
    return array.at[tuple(spot)].set(low).at[tuple(next_to)].set(largest)


def steps_of(key, extent, cuts, least, top_value):
    loudness = 1.0
    for axis_at, blocks in cuts:
        draws = jax.random.uniform(jax.random.fold_in(jax.random.fold_in(key, 6), axis_at), (blocks,), jnp.float32, least / len(cuts), top_value / len(cuts))
        loudness = loudness * jnp.repeat(jnp.exp(draws), extent[axis_at] // blocks).reshape((-1,) + (1,) * (len(extent) - 1 - axis_at))
    return loudness


def setup_inputs(seed: int = 0) -> dict:
    splits = jax.random.split(jax.random.key(seed), 7)
    action = jnp.clip(jnp.exp(math.log(1.0) - 2.3025851 * jax.random.uniform(splits[0], (NF, DIRS, NX, NR), jnp.float32) ** steps_of(splits[0], (NF, DIRS, NX, NR), ((0, 8), (2, 64)), -0.2, 0.2)), 0.1, 1.0)
    courant = jnp.clip(jnp.exp(math.log(0.6) - 1.7917595 * jax.random.uniform(splits[1], (NF,), jnp.float32) ** steps_of(splits[1], (NF,), ((0, 8),), -0.2, 0.2)), 0.1, 0.6)
    bending = jnp.clip(jax.random.uniform(splits[2], (NX, NR), jnp.float32, -0.25, 0.25) * steps_of(splits[2], (NX, NR), ((0, 64),), -0.4, 0.0), -0.25, 0.25)
    land_mask = set_ends((jax.random.randint(splits[3], (NX, NR), 0, 8) < 1).astype(jnp.int32), jax.random.fold_in(splits[3], 1), 0, 1)
    friction = jnp.clip(jnp.exp(math.log(2.0) - 1.3862944 * jax.random.uniform(splits[4], (NX, NR), jnp.float32) ** steps_of(splits[4], (NX, NR), ((0, 512),), -0.2, 0.2)), 0.5, 2.0)
    wind_dir = jnp.clip(jax.random.uniform(splits[5], (NX, NR), jnp.float32, -3.140625, 3.140625), -3.140625, 3.140625)
    return dict(action=action, courant=courant, bending=bending, land_mask=land_mask, friction=friction, wind_dir=wind_dir)


def advance_band(state, speed, bending, sea, thetas):
    speed_x = (speed * jnp.cos(thetas))[:, None, None]
    speed_y = (speed * jnp.sin(thetas))[:, None, None]
    turning = (bending * speed)[None, :, :]
    for substep in range(ITERS):
        west = jnp.roll(state, 1, axis=1)
        east = jnp.roll(state, -1, axis=1)
        south = jnp.pad(state, ((0, 0), (0, 0), (1, 0)))[:, :, :-1]
        north = jnp.pad(state, ((0, 0), (0, 0), (0, 1)))[:, :, 1:]
        before = jnp.roll(state, 1, axis=0)
        after = jnp.roll(state, -1, axis=0)
        change = jnp.maximum(speed_x, 0.0) * (state - west) + jnp.minimum(speed_x, 0.0) * (east - state)
        change = change + jnp.maximum(speed_y, 0.0) * (state - south) + jnp.minimum(speed_y, 0.0) * (north - state)
        change = change + jnp.maximum(turning, 0.0) * (state - before) + jnp.minimum(turning, 0.0) * (after - state)
        state = (state - change) * sea[None]
    return state


def reference(action, courant, bending, land_mask, friction, wind_dir):
    sea = (1 - land_mask).astype(jnp.float32)
    thetas = 2.0 * jnp.pi * jnp.arange(DIRS).astype(jnp.float32) / DIRS

    def one_band(items):
        band, speed = items
        return advance_band(band * sea[None], speed, bending, sea, thetas)

    state = lax.map(one_band, (action, courant))
    energy = jnp.sum(state, axis=(0, 1)) / (NF * DIRS)
    facing = jnp.maximum(jnp.cos(thetas[:, None, None] - wind_dir[None]), 0.0)
    zero_band = jnp.zeros_like(state[:1])
    lower_all = jnp.roll(jnp.concatenate((zero_band, state[:-1]), axis=0), -1, axis=1)
    upper_all = jnp.roll(jnp.concatenate((state[1:], zero_band), axis=0), 1, axis=1)

    def source_band(items):
        band, lower, upper, index = items
        ratio = (index + 1).astype(jnp.float32) / NF
        growth = 0.5 * friction[None] * ratio * facing
        coupling = 0.5 * (lower * upper - band * band)
        return (band * (1.0 + growth) + coupling) / (1.0 + 4.0 * ratio * ratio * energy * energy)[None]

    return lax.map(source_band, (state, lower_all, upper_all, jnp.arange(NF).astype(jnp.int32)))
```

```python
import functools

import jax
import jax.numpy as jnp
import numpy as np
from jax import lax
from jax.experimental import pallas as pl
from jax.experimental.pallas import tpu as pltpu
from jax.sharding import PartitionSpec as P

ITERS = 8
DIRS = 36
COLS = 32
HALF = DIRS // 2
ANGLES = 2.0 * np.pi * np.arange(DIRS) / DIRS
COS = [float(v) for v in np.cos(ANGLES)]
SIN = [float(v) for v in np.sin(ANGLES)]
EASTGOING = [d for d in range(DIRS) if COS[d] > 0.0]
WESTGOING = [d for d in range(DIRS) if COS[d] <= 0.0]
NORTHGOING = [SIN[d] >= 0.0 for d in range(DIRS)]
SLAB = COLS + 2 * ITERS
ROWS1 = DIRS * SLAB
TILES = HALF + HALF // 2 - 2
SPAN = DIRS * 2 * ITERS
WHOLE = pl.BlockSpec(memory_space=pltpu.VMEM)
SCALARS = pl.BlockSpec(memory_space=pltpu.SMEM)
PARAMS = pltpu.CompilerParams(vmem_limit_bytes=24 << 20)


def halo_plan(full):
    first = [d for d in full if (d - 1) % DIRS not in full][0]
    last = (first + HALF - 1) % DIRS
    up = [(last + 1 + j) % DIRS for j in range(HALF // 2)]
    down = [(first - 1 - j) % DIRS for j in range(HALF // 2)]
    pairs = [(0, up[0], up[6]), (1, up[1], up[5]), (2, up[2], up[4]), (3, up[3], down[3])]
    pairs += [(0, down[0], down[6]), (1, down[1], down[5]), (2, down[2], down[4])]
    unused = [up[7], up[8], down[7], down[8]]
    return [(first + i) % DIRS for i in range(HALF)], pairs, unused


def pack_kernel(
    courant_ref, action_hbm, *refs
):
    maps_hbm, (to_east_ref, to_west_ref, speed_ref, action_ref), maps_ref, (sems,) = (
        refs[:4], refs[4:8], refs[8:12], refs[12:]
    )
    row = lax.broadcasted_iota(jnp.int32, (ITERS, 128), 0)
    bands = action_ref.shape[0]
    copies = [pltpu.make_async_copy(action_hbm.at[f], action_ref.at[f], sems.at[f]) for f in range(bands)]
    maps = [pltpu.make_async_copy(src, dst, sems.at[bands + i]) for i, (src, dst) in enumerate(zip(maps_hbm, maps_ref))]
    for copy in copies + maps:
        copy.start()
    for f in range(bands):
        speed_ref[f] = jnp.full((ITERS, 128), courant_ref[f], jnp.float32)
    sides = (
        (to_east_ref, EASTGOING, False, slice(COLS - ITERS, COLS)),
        (to_west_ref, WESTGOING, True, slice(0, ITERS)),
    )
    for f in range(bands):
        copies[f].wait()
        for dst, full, flip, edge in sides:
            whole, pairs, _ = halo_plan(full)
            for t, d in enumerate(whole):
                dst[f * TILES + t] = action_ref[f, d, edge]
            for t, (j, one, two) in enumerate(pairs):
                a, b = action_ref[f, one, edge], action_ref[f, two, edge]
                if flip:
                    tile = jnp.where(row < ITERS - 1 - j, a, pltpu.roll(b, ITERS - 1 - j, 0))
                else:
                    tile = jnp.where(row > j, a, pltpu.roll(b, j + 1, 0))
                dst[f * TILES + HALF + t] = tile
    for copy in maps:
        copy.wait()
    bend_ref, land_ref = maps_ref[:2]
    for dst, _, _, edge in sides:
        dst[bands * TILES] = bend_ref[edge]
        dst[bands * TILES + 1] = 1.0 - land_ref[edge].astype(jnp.float32)


def pack(courant, action, *maps):
    bands = action.shape[0]
    halo = (bands * TILES + 2, ITERS, 128)
    in_hbm = pl.BlockSpec(memory_space=pltpu.MemorySpace.HBM)
    outs = [jax.ShapeDtypeStruct(o, jnp.float32) for o in (halo, halo, (bands, ITERS, 128), action.shape)]
    outs += [jax.ShapeDtypeStruct(x.shape, x.dtype) for x in maps]
    return pl.pallas_call(
        pack_kernel,
        in_specs=[SCALARS] + [in_hbm] * 5,
        out_specs=[WHOLE] * 8,
        out_shape=outs,
        scratch_shapes=[pltpu.SemaphoreType.DMA((bands + 4,))],
        compiler_params=PARAMS,
        name="pack",
    )(courant, action, *maps)


def weights(speed, d, lane):
    row_w = jnp.where(lane == (0 if NORTHGOING[d] else 127), 0.0, speed * abs(SIN[d]))
    return 1.0 - speed * (abs(COS[d]) + abs(SIN[d])), speed * abs(COS[d]), row_w


def band_of(role):
    odd = lax.rem(lax.axis_index("spec"), 2)
    return jnp.where(role == 0, 2 * odd, jnp.where(role == 1, 2 - 2 * odd, 1))


def rowwise(d, here):
    return pltpu.roll(here, 1 if NORTHGOING[d] else 127, 1)


def inner_kernel(
    speed_ref, action_ref, bend_ref, land_ref, far_ref, near_ref, own_ref, left, right, total_ref,
    st, own_c, col_c, row_c,
):
    lane = lax.broadcasted_iota(jnp.int32, (ITERS, 128), 1)
    blocks = COLS // ITERS
    part = [slice(ITERS * i, ITERS * (i + 1)) for i in range(blocks)]
    inside = [slice(ITERS * (i + 1), ITERS * (i + 2)) for i in range(blocks)]
    total_ref[...] = jnp.zeros_like(total_ref)

    def one_role(role, carry):
        band = band_of(role)
        speed = speed_ref[band]
        turn, positive = [], []
        sea = [1.0 - land_ref[p].astype(jnp.float32) for p in part]
        for i in range(blocks):
            bend = bend_ref[part[i]]
            turn.append(jnp.abs(bend * speed) * sea[i])
            positive.append(bend > 0.0)
        for d in range(DIRS):
            own_w, col_w, row_w = weights(speed, d, lane)
            for i in range(blocks):
                own_c[d, part[i]] = own_w - turn[i]
                col_c[d, part[i]] = col_w * sea[i]
                row_c[d, part[i]] = row_w * sea[i]
                st[0, d, inside[i]] = action_ref[band, d, part[i]] * sea[i]

        def load(k, d, shift):
            return [st[k, d, slice(p.start + shift, p.stop + shift)] for p in inside]

        def substep(k, carry):
            before = load(k, DIRS - 1, 0)
            here = load(k, 0, 0)
            for d in range(DIRS):
                after = load(k, (d + 1) % DIRS, 0)
                upwind = load(k, d, -1 if d in EASTGOING else 1)
                for i in range(blocks):
                    kept = own_c[d, part[i]] * here[i] + turn[i] * jnp.where(positive[i], before[i], after[i])
                    moved = col_c[d, part[i]] * upwind[i] + row_c[d, part[i]] * rowwise(d, here[i])
                    st[k + 1, d, inside[i]] = kept + moved
                before, here = here, after
            return carry

        lax.fori_loop(0, ITERS, substep, 0)
        flat = st.reshape((ITERS + 1) * ROWS1, 128)
        lflat, rflat = left.at[role].reshape((ITERS + 1) * SPAN, 128), right.at[role].reshape((ITERS + 1) * SPAN, 128)
        for d in range(DIRS):
            base, strip = d * SLAB + ITERS, d * 2 * ITERS
            lflat[pl.ds(strip + ITERS, ITERS, stride=SPAN), :] = flat[pl.ds(base, ITERS, stride=ROWS1 + 1), :]
            rflat[pl.ds(strip + ITERS - 1, ITERS, stride=SPAN), :] = flat[
                pl.ds(base + COLS - 1, ITERS, stride=ROWS1 - 1), :
            ]
            if d in WESTGOING:
                lflat[pl.ds(strip + ITERS + 1, ITERS, stride=SPAN), :] = flat[
                    pl.ds(base + 1, ITERS, stride=ROWS1 + 1), :
                ]
            else:
                rflat[pl.ds(strip + ITERS - 2, ITERS, stride=SPAN), :] = flat[
                    pl.ds(base + COLS - 2, ITERS, stride=ROWS1 - 1), :
                ]
        for r, out in enumerate((far_ref, near_ref, own_ref)):

            @pl.when(role == r)
            def _(out=out):
                sums = [total_ref[p] for p in part[1:3]]
                for d in range(DIRS):
                    for i in range(2):
                        value = st[ITERS, d, inside[i + 1]]
                        out[d, part[i + 1]] = value
                        sums[i] = sums[i] + value
                for i in range(2):
                    total_ref[part[i + 1]] = sums[i]

        return carry

    lax.fori_loop(0, action_ref.shape[0], one_role, 0)


def inner(speed, action, bending, land_mask):
    bands = action.shape[0]
    state = (DIRS, COLS, 128)
    strip = (bands, ITERS + 1, DIRS, 2 * ITERS, 128)
    return pl.pallas_call(
        inner_kernel,
        in_specs=[WHOLE] * 4,
        out_specs=[WHOLE] * 6,
        out_shape=[jax.ShapeDtypeStruct(o, jnp.float32) for o in (state, state, state, strip, strip, (COLS, 128))],
        scratch_shapes=[pltpu.VMEM((ITERS + 1, DIRS, SLAB, 128), jnp.float32)]
        + [pltpu.VMEM((DIRS, COLS, 128), jnp.float32)] * 3,
        cost_estimate=pl.CostEstimate(flops=40_000_000, bytes_accessed=6_000_000, transcendentals=0),
        compiler_params=PARAMS,
        name="inner",
    )(speed, action, bending, land_mask)


def strips_kernel(
    speed_ref, west_ref, east_ref, bend_ref, land_ref, friction_ref, wind_ref,
    far_in, near_in, own_in, left_in, right_in, total_in,
    far_ref, near_ref, own_ref, left_all, right_all, total, pay_ref, own_c, col_c, row_c, sea_ext, bend_ext,
):
    lane = lax.broadcasted_iota(jnp.int32, (ITERS, 128), 1)
    bands = left_all.shape[0]
    extra = west_ref.shape[0] - 2
    bend_ext[:ITERS] = west_ref[extra]
    bend_ext[ITERS : ITERS + COLS] = bend_ref[...]
    bend_ext[ITERS + COLS :] = east_ref[extra]
    sea_ext[:ITERS] = west_ref[extra + 1]
    sea_ext[ITERS : ITERS + COLS] = 1.0 - land_ref[...].astype(jnp.float32)
    sea_ext[ITERS + COLS :] = east_ref[extra + 1]
    zero = jnp.zeros((ITERS, 128), jnp.float32)

    def one_role(role, carry):
        band = band_of(role)
        speed = speed_ref[band]
        left, right = left_all.at[role], right_all.at[role]
        for d in range(DIRS):
            own_c[d], col_c[d], row_c[d] = weights(speed, d, lane)
        for src, buf, full, flip, row0 in (
            (west_ref, left, EASTGOING, False, 0),
            (east_ref, right, WESTGOING, True, ITERS),
        ):
            whole, pairs, unused = halo_plan(full)
            sea = src[extra + 1]
            rows = slice(row0, row0 + ITERS)
            for t, d in enumerate(whole):
                buf[0, d, rows] = src[band * TILES + t] * sea
            for t, (j, one, two) in enumerate(pairs):
                tile = src[band * TILES + HALF + t]
                buf[0, one, rows] = tile * sea
                buf[0, two, rows] = pltpu.roll(tile, j + 1 if flip else ITERS - 1 - j, 0) * sea
            for d in unused:
                buf[0, d, rows] = zero

        for k in range(ITERS):
            sides = []
            for buf, center, row0, window in (
                (left, 1, 0, k + 1),
                (right, ITERS - 1, ITERS, ITERS + COLS - 1 - k),
            ):
                s = sea_ext[window : window + ITERS]
                bend = bend_ext[window : window + ITERS]
                turn = jnp.abs(bend * speed) * s
                load = functools.partial(lambda buf, d, at: buf[k, d, at : at + ITERS], buf)
                sides.append([buf, center, row0, s, turn, bend > 0.0, load, load(DIRS - 1, center), load(0, center)])
            for d in range(DIRS):
                own_w, col_w, row_w = own_c[d], col_c[d], row_c[d]
                for side in sides:
                    buf, center, row0, s, turn, positive, load, before, here = side
                    after = load((d + 1) % DIRS, center)
                    upwind = load(d, center + (-1 if d in EASTGOING else 1))
                    moved = own_w * here + col_w * upwind + row_w * rowwise(d, here)
                    new = s * moved + turn * (jnp.where(positive, before, after) - here)
                    buf[k + 1, d, row0 : row0 + ITERS] = new
                    side[7], side[8] = here, after

        ends = (slice(0, ITERS), slice(COLS - ITERS, COLS))
        for r, out in enumerate((far_ref, near_ref, own_ref)):

            @pl.when(role == r)
            def _(out=out):
                sums = [total[p] for p in ends]
                for d in range(DIRS):
                    for i, value in enumerate((left[ITERS, d, :ITERS], right[ITERS, d, ITERS:])):
                        out[d, ends[i]] = value
                        sums[i] = sums[i] + value
                for i in range(2):
                    total[ends[i]] = sums[i]

        return carry

    lax.fori_loop(0, bands, one_role, 0)
    quarter = friction_ref.shape[0]
    for peer in range(pay_ref.shape[0]):
        pay_ref[peer, :COLS] = total[...]
        pay_ref[peer, COLS : COLS + quarter] = friction_ref[...]
        pay_ref[peer, COLS + quarter :] = wind_ref[...]


def strips(speed, west, east, kept, bending, land_mask, friction, wind_dir, peers):
    pay = jax.ShapeDtypeStruct((peers, COLS + 2 * friction.shape[0], 128), jnp.float32)
    outs = pl.pallas_call(
        strips_kernel,
        in_specs=[WHOLE] * 13,
        out_specs=[WHOLE] * 7,
        out_shape=[jax.ShapeDtypeStruct(x.shape, x.dtype) for x in kept] + [pay],
        input_output_aliases={7 + i: i for i in range(6)},
        scratch_shapes=[
            pltpu.VMEM((DIRS, ITERS, 128), jnp.float32),
            pltpu.VMEM((DIRS, ITERS, 128), jnp.float32),
            pltpu.VMEM((DIRS, ITERS, 128), jnp.float32),
            pltpu.VMEM((COLS + 2 * ITERS, 128), jnp.float32),
            pltpu.VMEM((COLS + 2 * ITERS, 128), jnp.float32),
        ],
        compiler_params=PARAMS,
        name="strips",
    )(speed, west, east, bending, land_mask, friction, wind_dir, *kept)
    return outs[0], outs[1], outs[2], outs[6]


def finish_kernel(far_ref, near_ref, own_ref, far_in_ref, near_in_ref, pay_ref, out_hbm, out_ref, sems):
    peers = pay_ref.shape[0]
    here = lax.axis_index("spec")
    odd = lax.rem(here, 2)
    bands = out_ref.shape[0]
    total_bands = bands * peers
    row = lax.broadcasted_iota(jnp.int32, (ITERS, 128), 0)
    part = [slice(ITERS * i, ITERS * (i + 1)) for i in range(COLS // ITERS)]
    along, across, energy2 = [], [], []
    for i, p in enumerate(part):
        energy = pay_ref[0, p]
        for peer in range(1, peers):
            energy = energy + pay_ref[peer, p]
        energy = energy / float(total_bands * DIRS)
        energy2.append(4.0 * energy * energy)
        lower_half, upper_half = pay_ref[2 * i, COLS:], pay_ref[2 * i + 1, COLS:]
        friction = jnp.where(row < 4, lower_half, pltpu.roll(upper_half, 4, 0))
        wind = jnp.where(row < 4, pltpu.roll(lower_half, 4, 0), upper_half)
        along.append(friction * jnp.cos(wind))
        across.append(friction * jnp.sin(wind))
    chunk = DIRS // sems.shape[1]

    def send(f, c):
        at = pl.ds(c * chunk, chunk)
        return pltpu.make_async_copy(out_ref.at[f, at], out_hbm.at[f, at], sems.at[f, c])

    for parity in (0, 1):

        @pl.when(odd == parity)
        def _(step=2 * parity - 1, order=(2 * parity, 2 - 2 * parity, 1)):
            plan = []
            for band in order:
                g = (here * bands + band + 1).astype(jnp.float32) / float(total_bands)
                plan.append((band, g, [0.5 / (1.0 + (g * g) * e) for e in energy2]))
            for d in range(DIRS):
                plus, minus = (d + step) % DIRS, (d - step) % DIRS
                for i, p in enumerate(part):
                    facing = jnp.maximum(COS[d] * along[i] + SIN[d] * across[i], 0.0)
                    pairs = (
                        (far_ref[d, p], own_ref[plus, p] * far_in_ref[minus, p]),
                        (near_ref[d, p], own_ref[minus, p] * near_in_ref[plus, p]),
                        (own_ref[d, p], far_ref[minus, p] * near_ref[plus, p]),
                    )
                    for (value, product), (band, g, scale) in zip(pairs, plan):
                        out_ref[band, d, p] = (value * (2.0 + g * facing - value) + product) * scale[i]
                if d % chunk == chunk - 1:
                    for f in range(bands):
                        send(f, d // chunk).start()

    for f in range(bands):
        for c in range(sems.shape[1]):
            send(f, c).wait()


def finish(far, near, own, far_in, near_in, pay, bands):
    out = (bands, DIRS, COLS, 128)
    return pl.pallas_call(
        finish_kernel,
        in_specs=[WHOLE] * 6,
        out_specs=pl.BlockSpec(memory_space=pltpu.MemorySpace.HBM),
        out_shape=jax.ShapeDtypeStruct(out, jnp.float32),
        scratch_shapes=[pltpu.VMEM(out, jnp.float32), pltpu.SemaphoreType.DMA((bands, 4))],
        compiler_params=PARAMS,
        name="finish",
    )(far, near, own, far_in, near_in, pay)


def shards(action, courant, bending, land_mask, friction, wind_dir):
    bands = action.shape[0]
    peers = lax.axis_size("spec")
    tiles = lax.axis_size("space")
    in_hbm = lambda x: pltpu.with_memory_space_constraint(x, pltpu.MemorySpace.HBM)
    to_east, to_west, speed, action, bending, land_mask, friction, wind_dir = pack(
        *map(in_hbm, (courant, action, bending, land_mask, friction, wind_dir))
    )
    ring = [(i, (i + 1) % tiles) for i in range(tiles)]
    west = lax.ppermute(to_east, "space", ring)
    east = lax.ppermute(to_west, "space", [(b, a) for a, b in ring])
    kept = inner(speed, action, bending, land_mask)
    far, near, own, pay = strips(speed, west, east, kept, bending, land_mask, friction, wind_dir, peers)
    far_pairs = [(i, i + 1) for i in range(1, peers - 1, 2)]
    near_pairs = [(i, i + 1) for i in range(0, peers, 2)]
    far_in = lax.ppermute(far, "spec", far_pairs + [(b, a) for a, b in far_pairs])
    near_in = lax.ppermute(near, "spec", near_pairs + [(b, a) for a, b in near_pairs])
    pay = pltpu.with_memory_space_constraint(pay, pltpu.MemorySpace.VMEM)
    pay = lax.all_to_all(pay, "spec", split_axis=0, concat_axis=0, tiled=True)
    return finish(far, near, own, far_in, near_in, pay, bands)


def solution(mesh):
    return jax.shard_map(
        shards,
        mesh=mesh,
        in_specs=(
            P("spec", None, "space", None),
            P("spec"),
            P("space", None),
            P("space", None),
            P(("space", "spec"), None),
            P(("space", "spec"), None),
        ),
        out_specs=P("spec", None, "space", None),
        check_vma=False,
    )
```

```python
import functools

import jax
import jax.numpy as jnp
import numpy as np
from jax import lax
from jax.experimental import pallas as pl
from jax.experimental.pallas import tpu as pltpu
from jax.sharding import PartitionSpec as P

ITERS = 8
DIRS = 36
COLS = 32
HALF = DIRS // 2
ANGLES = 2.0 * np.pi * np.arange(DIRS) / DIRS
COS = [float(v) for v in np.cos(ANGLES)]
SIN = [float(v) for v in np.sin(ANGLES)]
EASTGOING = [d for d in range(DIRS) if COS[d] > 0.0]
WESTGOING = [d for d in range(DIRS) if COS[d] <= 0.0]
NORTHGOING = [SIN[d] >= 0.0 for d in range(DIRS)]
SLAB = COLS + 2 * ITERS
TILES = HALF + HALF // 2 - 2
WHOLE = pl.BlockSpec(memory_space=pltpu.VMEM)
PARAMS = pltpu.CompilerParams(vmem_limit_bytes=24 << 20)
PACKED = pltpu.CompilerParams(vmem_limit_bytes=24 << 20)


def halo_plan(full):
    first = [d for d in full if (d - 1) % DIRS not in full][0]
    last = (first + HALF - 1) % DIRS
    up = [(last + 1 + j) % DIRS for j in range(HALF // 2)]
    down = [(first - 1 - j) % DIRS for j in range(HALF // 2)]
    pairs = [(0, up[0], up[6]), (1, up[1], up[5]), (2, up[2], up[4]), (3, up[3], down[3])]
    pairs += [(0, down[0], down[6]), (1, down[1], down[5]), (2, down[2], down[4])]
    return [(first + i) % DIRS for i in range(HALF)], pairs


def beyond(d, full):
    if d in full:
        return -1
    return [any((d + s * (j + 1)) % DIRS in full for s in (-1, 1)) for j in range(HALF)].index(True)


def pack_kernel(
    courant_hbm, action_hbm, *refs
):
    maps_hbm, (to_east_ref, to_west_ref, speed_ref, action_ref), maps_ref, (courant_ref, sems) = (
        refs[:4], refs[4:8], refs[8:12], refs[12:]
    )
    row = lax.broadcasted_iota(jnp.int32, (ITERS, 128), 0)
    bands = action_ref.shape[0]
    copies = [pltpu.make_async_copy(action_hbm.at[f], action_ref.at[f], sems.at[f]) for f in range(bands)]
    maps = [pltpu.make_async_copy(src, dst, sems.at[bands + i]) for i, (src, dst) in enumerate(zip(maps_hbm, maps_ref))]
    maps.append(pltpu.make_async_copy(courant_hbm, courant_ref, sems.at[bands + 4]))
    for copy in copies + maps:
        copy.start()
    sides = (
        (to_east_ref, EASTGOING, False, slice(COLS - ITERS, COLS)),
        (to_west_ref, WESTGOING, True, slice(0, ITERS)),
    )
    for f in range(bands):
        copies[f].wait()
        for dst, full, flip, edge in sides:
            whole, pairs = halo_plan(full)
            for t, d in enumerate(whole):
                dst[f * TILES + t] = action_ref[f, d, edge]
            for t, (j, one, two) in enumerate(pairs):
                a, b = action_ref[f, one, edge], action_ref[f, two, edge]
                if flip:
                    tile = jnp.where(row < ITERS - 1 - j, a, pltpu.roll(b, ITERS - 1 - j, 0))
                else:
                    tile = jnp.where(row > j, a, pltpu.roll(b, j + 1, 0))
                dst[f * TILES + HALF + t] = tile
    for copy in maps:
        copy.wait()
    for f in range(bands):
        speed_ref[f] = jnp.full((ITERS, 128), courant_ref[f], jnp.float32)
    bend_ref, land_ref = maps_ref[:2]
    for dst, _, _, edge in sides:
        dst[bands * TILES] = bend_ref[edge]
        dst[bands * TILES + 1] = 1.0 - land_ref[edge].astype(jnp.float32)


def pack(courant, action, *maps):
    bands = action.shape[0]
    halo = (bands * TILES + 2, ITERS, 128)
    in_hbm = pl.BlockSpec(memory_space=pltpu.MemorySpace.HBM)
    outs = [jax.ShapeDtypeStruct(o, jnp.float32) for o in (halo, halo, (bands, ITERS, 128), action.shape)]
    outs += [jax.ShapeDtypeStruct(x.shape, x.dtype) for x in maps]
    return pl.pallas_call(
        pack_kernel,
        in_specs=[in_hbm] * 6,
        out_specs=[WHOLE] * 8,
        out_shape=outs,
        scratch_shapes=[pltpu.SMEM((bands,), jnp.float32), pltpu.SemaphoreType.DMA((bands + 5,))],
        compiler_params=PARAMS,
        name="pack",
    )(courant, action, *maps)


def weights(speed, d, lane):
    row_w = jnp.where(lane == (0 if NORTHGOING[d] else 127), 0.0, speed * abs(SIN[d]))
    return 1.0 - speed * (abs(COS[d]) + abs(SIN[d])), speed * abs(COS[d]), row_w


def band_of(role):
    odd = lax.rem(lax.axis_index("spec"), 2)
    return jnp.where(role == 0, 2 * odd, jnp.where(role == 1, 2 - 2 * odd, 1))


def rowwise(d, here):
    return pltpu.roll(here, 1 if NORTHGOING[d] else 127, 1)


def inner_kernel(
    speed_ref, action_ref, bend_ref, land_ref, far_ref, near_ref, own_ref, left, right, total_ref,
    st, own_c, col_c, row_c,
):
    lane = lax.broadcasted_iota(jnp.int32, (ITERS, 128), 1)
    blocks = COLS // ITERS
    part = [slice(ITERS * i, ITERS * (i + 1)) for i in range(blocks)]
    inside = [slice(ITERS * (i + 1), ITERS * (i + 2)) for i in range(blocks)]
    total_ref[...] = jnp.zeros_like(total_ref)

    def one_role(role, carry):
        band = band_of(role)
        speed = speed_ref[band]
        turn, positive = [], []
        sea = [1.0 - land_ref[p].astype(jnp.float32) for p in part]
        for i in range(blocks):
            bend = bend_ref[part[i]]
            turn.append(jnp.abs(bend * speed) * sea[i])
            positive.append(bend > 0.0)
        for d in range(DIRS):
            own_w, col_w, row_w = weights(speed, d, lane)
            for i in range(blocks):
                own_c[d, part[i]] = own_w - turn[i]
                col_c[d, part[i]] = col_w * sea[i]
                row_c[d, part[i]] = row_w * sea[i]
                value = action_ref[band, d, part[i]] * sea[i]
                st[0, d, inside[i]] = value
                if i == 0:
                    left[role, 0, d, ITERS:] = value
                if i == blocks - 1:
                    right[role, 0, d, :ITERS] = value

        def load(k, d, shift):
            return [st[k, d, slice(p.start + shift, p.stop + shift)] for p in inside]

        def substep(k, carry):
            before = load(k, DIRS - 1, 0)
            here = load(k, 0, 0)
            for d in range(DIRS):
                after = load(k, (d + 1) % DIRS, 0)
                upwind = load(k, d, -1 if d in EASTGOING else 1)
                for i in range(blocks):
                    kept = own_c[d, part[i]] * here[i] + turn[i] * jnp.where(positive[i], before[i], after[i])
                    moved = col_c[d, part[i]] * upwind[i] + row_c[d, part[i]] * rowwise(d, here[i])
                    value = kept + moved
                    st[k + 1, d, inside[i]] = value
                    if i == 0:
                        left[role, k + 1, d, pl.ds(ITERS - 1 - k, ITERS)] = value
                    if i == blocks - 1:
                        right[role, k + 1, d, pl.ds(k + 1, ITERS)] = value
                before, here = here, after
            return carry

        lax.fori_loop(0, ITERS, substep, 0)
        for d in range(DIRS):
            if d in WESTGOING:
                left[role, ITERS - 1, d, ITERS + 1 : ITERS + 2] = st[ITERS - 1, d, 2 * ITERS : 2 * ITERS + 1]
            else:
                right[role, ITERS - 1, d, ITERS - 2 : ITERS - 1] = st[ITERS - 1, d, COLS - 1 : COLS]
        for r, out in enumerate((far_ref, near_ref, own_ref)):

            @pl.when(role == r)
            def _(out=out):
                sums = [total_ref[p] for p in part[1:3]]
                for d in range(DIRS):
                    for i in range(2):
                        value = st[ITERS, d, inside[i + 1]]
                        out[d, part[i + 1]] = value
                        sums[i] = sums[i] + value
                for i in range(2):
                    total_ref[part[i + 1]] = sums[i]

        return carry

    lax.fori_loop(0, action_ref.shape[0], one_role, 0)


def inner(speed, action, bending, land_mask):
    bands = action.shape[0]
    state = (DIRS, COLS, 128)
    strip = (bands, ITERS + 1, DIRS, 2 * ITERS, 128)
    return pl.pallas_call(
        inner_kernel,
        in_specs=[WHOLE] * 4,
        out_specs=[WHOLE] * 6,
        out_shape=[jax.ShapeDtypeStruct(o, jnp.float32) for o in (state, state, state, strip, strip, (COLS, 128))],
        scratch_shapes=[pltpu.VMEM((ITERS + 1, DIRS, SLAB, 128), jnp.float32)]
        + [pltpu.VMEM((DIRS, COLS, 128), jnp.float32)] * 3,
        cost_estimate=pl.CostEstimate(flops=40_000_000, bytes_accessed=6_000_000, transcendentals=0),
        compiler_params=PACKED,
        name="inner",
    )(speed, action, bending, land_mask)


def strips_kernel(
    speed_ref, west_ref, east_ref, bend_ref, land_ref, friction_ref, wind_ref,
    far_in, near_in, own_in, left_in, right_in, total_in,
    far_ref, near_ref, own_ref, left_all, right_all, total, pay_ref, own_c, col_c, row_c, sea_ext, bend_ext,
):
    lane = lax.broadcasted_iota(jnp.int32, (ITERS, 128), 1)
    bands = left_all.shape[0]
    extra = west_ref.shape[0] - 2
    bend_ext[:ITERS] = west_ref[extra]
    bend_ext[ITERS : ITERS + COLS] = bend_ref[...]
    bend_ext[ITERS + COLS :] = east_ref[extra]
    sea_ext[:ITERS] = west_ref[extra + 1]
    sea_ext[ITERS : ITERS + COLS] = 1.0 - land_ref[...].astype(jnp.float32)
    sea_ext[ITERS + COLS :] = east_ref[extra + 1]
    def one_role(role, carry):
        band = band_of(role)
        speed = speed_ref[band]
        left, right = left_all.at[role], right_all.at[role]
        for d in range(DIRS):
            own_c[d], col_c[d], row_c[d] = weights(speed, d, lane)
        for src, buf, full, flip, row0 in (
            (west_ref, left, EASTGOING, False, 0),
            (east_ref, right, WESTGOING, True, ITERS),
        ):
            whole, pairs = halo_plan(full)
            sea = src[extra + 1]
            rows = slice(row0, row0 + ITERS)
            for t, d in enumerate(whole):
                buf[0, d, rows] = src[band * TILES + t] * sea
            for t, (j, one, two) in enumerate(pairs):
                tile = src[band * TILES + HALF + t]
                buf[0, one, rows] = tile * sea
                buf[0, two, rows] = pltpu.roll(tile, j + 1 if flip else ITERS - 1 - j, 0) * sea

        for k in range(ITERS):
            for buf, center, row0, window, full in (
                (left, 1, 0, k + 1, EASTGOING),
                (right, ITERS - 1, ITERS, ITERS + COLS - 1 - k, WESTGOING),
            ):
                s = sea_ext[window : window + ITERS]
                bend = bend_ext[window : window + ITERS]
                turn = jnp.abs(bend * speed) * s
                load = functools.partial(lambda buf, d, at: buf[k, d, at : at + ITERS], buf)
                late = max(ITERS - 2 - k, k)
                for d in range(DIRS):
                    if beyond(d, full) >= late:
                        continue
                    here, upwind = load(d, center), load(d, center + (-1 if d in EASTGOING else 1))
                    before, after = load((d - 1) % DIRS, center), load((d + 1) % DIRS, center)
                    moved = own_c[d] * here + col_c[d] * upwind + row_c[d] * rowwise(d, here)
                    new = s * moved + turn * (jnp.where(bend > 0.0, before, after) - here)
                    buf[k + 1, d, row0 : row0 + ITERS] = new

        ends = (slice(0, ITERS), slice(COLS - ITERS, COLS))
        for r, out in enumerate((far_ref, near_ref, own_ref)):

            @pl.when(role == r)
            def _(out=out):
                sums = [total[p] for p in ends]
                for d in range(DIRS):
                    for i, value in enumerate((left[ITERS, d, :ITERS], right[ITERS, d, ITERS:])):
                        out[d, ends[i]] = value
                        sums[i] = sums[i] + value
                for i in range(2):
                    total[ends[i]] = sums[i]

        return carry

    lax.fori_loop(0, bands, one_role, 0)
    quarter = friction_ref.shape[0]
    for peer in range(pay_ref.shape[0]):
        pay_ref[peer, :COLS] = total[...]
        pay_ref[peer, COLS : COLS + quarter] = friction_ref[...]
        pay_ref[peer, COLS + quarter :] = wind_ref[...]


def strips(speed, west, east, kept, bending, land_mask, friction, wind_dir, peers):
    pay = jax.ShapeDtypeStruct((peers, COLS + 2 * friction.shape[0], 128), jnp.float32)
    outs = pl.pallas_call(
        strips_kernel,
        in_specs=[WHOLE] * 13,
        out_specs=[WHOLE] * 7,
        out_shape=[jax.ShapeDtypeStruct(x.shape, x.dtype) for x in kept] + [pay],
        input_output_aliases={7 + i: i for i in range(6)},
        scratch_shapes=[
            pltpu.VMEM((DIRS, ITERS, 128), jnp.float32),
            pltpu.VMEM((DIRS, ITERS, 128), jnp.float32),
            pltpu.VMEM((DIRS, ITERS, 128), jnp.float32),
            pltpu.VMEM((COLS + 2 * ITERS, 128), jnp.float32),
            pltpu.VMEM((COLS + 2 * ITERS, 128), jnp.float32),
        ],
        compiler_params=PACKED,
        name="strips",
    )(speed, west, east, bending, land_mask, friction, wind_dir, *kept)
    return outs[0], outs[1], outs[2], outs[6]


def finish_kernel(far_ref, near_ref, own_ref, far_in_ref, near_in_ref, pay_ref, out_hbm, out_ref, sems):
    peers = pay_ref.shape[0]
    here = lax.axis_index("spec")
    odd = lax.rem(here, 2)
    bands = out_ref.shape[0]
    total_bands = bands * peers
    row = lax.broadcasted_iota(jnp.int32, (ITERS, 128), 0)
    part = [slice(ITERS * i, ITERS * (i + 1)) for i in range(COLS // ITERS)]
    along, across, energy2 = [], [], []
    for i, p in enumerate(part):
        energy = pay_ref[0, p]
        for peer in range(1, peers):
            energy = energy + pay_ref[peer, p]
        energy = energy / float(total_bands * DIRS)
        energy2.append(4.0 * energy * energy)
        lower_half, upper_half = pay_ref[2 * i, COLS:], pay_ref[2 * i + 1, COLS:]
        friction = jnp.where(row < 4, lower_half, pltpu.roll(upper_half, 4, 0))
        wind = jnp.where(row < 4, pltpu.roll(lower_half, 4, 0), upper_half)
        along.append(friction * jnp.cos(wind))
        across.append(friction * jnp.sin(wind))
    chunk = DIRS // sems.shape[1]

    def send(f, c):
        at = pl.ds(c * chunk, chunk)
        return pltpu.make_async_copy(out_ref.at[f, at], out_hbm.at[f, at], sems.at[f, c])

    for parity in (0, 1):

        @pl.when(odd == parity)
        def _(step=2 * parity - 1, order=(2 * parity, 2 - 2 * parity, 1)):
            plan = []
            for band in order:
                g = (here * bands + band + 1).astype(jnp.float32) / float(total_bands)
                plan.append((band, g, [0.5 / (1.0 + (g * g) * e) for e in energy2]))
            for d in range(DIRS):
                plus, minus = (d + step) % DIRS, (d - step) % DIRS
                for i, p in enumerate(part):
                    facing = jnp.maximum(COS[d] * along[i] + SIN[d] * across[i], 0.0)
                    pairs = (
                        (far_ref[d, p], own_ref[plus, p] * far_in_ref[minus, p]),
                        (near_ref[d, p], own_ref[minus, p] * near_in_ref[plus, p]),
                        (own_ref[d, p], far_ref[minus, p] * near_ref[plus, p]),
                    )
                    for (value, product), (band, g, scale) in zip(pairs, plan):
                        out_ref[band, d, p] = (value * (2.0 + g * facing - value) + product) * scale[i]
                if d % chunk == chunk - 1:
                    for f in range(bands):
                        send(f, d // chunk).start()

    for f in range(bands):
        for c in range(sems.shape[1]):
            send(f, c).wait()


def finish(far, near, own, far_in, near_in, pay, bands):
    out = (bands, DIRS, COLS, 128)
    return pl.pallas_call(
        finish_kernel,
        in_specs=[WHOLE] * 6,
        out_specs=pl.BlockSpec(memory_space=pltpu.MemorySpace.HBM),
        out_shape=jax.ShapeDtypeStruct(out, jnp.float32),
        scratch_shapes=[pltpu.VMEM(out, jnp.float32), pltpu.SemaphoreType.DMA((bands, 4))],
        compiler_params=PARAMS,
        name="finish",
    )(far, near, own, far_in, near_in, pay)


def shards(action, courant, bending, land_mask, friction, wind_dir):
    bands = action.shape[0]
    peers = lax.axis_size("spec")
    tiles = lax.axis_size("space")
    in_hbm = lambda x: pltpu.with_memory_space_constraint(x, pltpu.MemorySpace.HBM)
    to_east, to_west, speed, action, bending, land_mask, friction, wind_dir = pack(
        *map(in_hbm, (courant, action, bending, land_mask, friction, wind_dir))
    )
    ring = [(i, (i + 1) % tiles) for i in range(tiles)]
    west = lax.ppermute(to_east, "space", ring)
    east = lax.ppermute(to_west, "space", [(b, a) for a, b in ring])
    kept = inner(speed, action, bending, land_mask)
    far, near, own, pay = strips(speed, west, east, kept, bending, land_mask, friction, wind_dir, peers)
    far_pairs = [(i, i + 1) for i in range(1, peers - 1, 2)]
    near_pairs = [(i, i + 1) for i in range(0, peers, 2)]
    far_in = lax.ppermute(far, "spec", far_pairs + [(b, a) for a, b in far_pairs])
    near_in = lax.ppermute(near, "spec", near_pairs + [(b, a) for a, b in near_pairs])
    pay = pltpu.with_memory_space_constraint(pay, pltpu.MemorySpace.VMEM)
    pay = lax.all_to_all(pay, "spec", split_axis=0, concat_axis=0, tiled=True)
    return finish(far, near, own, far_in, near_in, pay, bands)


def solution(mesh):
    return jax.shard_map(
        shards,
        mesh=mesh,
        in_specs=(
            P("spec", None, "space", None),
            P("spec"),
            P("space", None),
            P("space", None),
            P(("space", "spec"), None),
            P(("space", "spec"), None),
        ),
        out_specs=P("spec", None, "space", None),
        check_vma=False,
    )
```
